256 devices in a mesh: mem: 32 (over x, y, core), lat: 8 (over z).
Axes of the slice: x: 4, y: 4, z: 8, core: 2. Of those that a mesh axis runs over, the one named last changes fastest.
Arguments:
- perturb: bfloat16 [128, 4, 256, 1024], P('mem', None, 'lat'), may hold values from -16 to 16
- gradient: float32 [4, 256, 1024], P(None, 'lat', 'mem'), may hold values from -6 to 6
- k_north: float32 [4, 256, 1024], P(None, 'lat'), may hold values from 0.1 to 0.35
- k_east: float32 [4, 256, 1024], P(None, 'lat'), may hold values from 0.02 to 0.15
- scale: float32 [4, 256, 1024], P(None, 'lat'), may hold values from 0.25 to 1
Outputs:
- product: float32 [4, 256, 1024], P(None, 'lat', 'mem')
The draws below stay inside these ranges and needn't reach their ends.
All inputs are finite; a program needn't handle non-finite values.
Results may differ from the reference program's by a relative error of at most 0.0003.
Values sent between devices are 32-bit elements; how exact they have to be, the bound alone decides.
No kernel may reach another device: no remote copies, remote signals or barrier semaphores. Data moves between devices by JAX's collectives and lax.ppermute only.
A program may use at most 128 MiB of HBM per device.

```python
import math
import jax
import jax.numpy as jnp
from jax import lax

MEM_DEV = 4
LEV = 4
LON = 1024
SWEEP = 4
MEMBERS = 128
LAT = 256
N_MEM = 32


def block_scale(stream_key, dims, cuts, low, high):
    def one(dim, parts):
        heights = jax.random.uniform(jax.random.fold_in(jax.random.fold_in(stream_key, 6), dim), (parts,), jnp.float32, low / len(cuts), high / len(cuts))
        return jnp.repeat(jnp.exp(heights), dims[dim] // parts).reshape((-1,) + (1,) * (len(dims) - dim - 1))

    level = one(*cuts[0])
    for cut in cuts[1:]:
        level = level * one(*cut)
    return level


def bell_draw(stream_key, extent, deviation, reach, shards=(), held_as=jnp.bfloat16):
    values = deviation * jax.random.normal(stream_key, extent, jnp.float32)
    if shards:
        values = values * block_scale(stream_key, extent, shards, -0.22, 0.18)
    return jnp.clip(values, -reach, reach).astype(held_as)


def setup_inputs(seed: int = 0) -> dict:
    arg_keys = jax.random.split(jax.random.key(seed), 6)
    perturb = bell_draw(arg_keys[0], (MEMBERS, LEV, LAT, LON), 4.0, 16.0, ((0, 32), (2, 8)))
    gradient = bell_draw(arg_keys[1], (LEV, LAT, LON), 1.0, 6.0, ((1, 8), (2, 32)), jnp.float32)
    k_north = jnp.clip(0.1 + 0.25 * jax.random.uniform(arg_keys[2], (LEV, LAT, LON), jnp.float32) ** block_scale(arg_keys[2], (LEV, LAT, LON), ((1, 8),), -0.2, 0.2), 0.1, 0.35)
    k_east = jnp.clip(0.02 + 0.13000001 * jax.random.uniform(arg_keys[3], (LEV, LAT, LON), jnp.float32) ** block_scale(arg_keys[3], (LEV, LAT, LON), ((1, 8),), -0.2, 0.2), 0.02, 0.15)
    scale = jnp.clip(jnp.exp(math.log(1.0) - 1.3862944 * jax.random.uniform(arg_keys[4], (LEV, LAT, LON), jnp.float32) ** block_scale(arg_keys[4], (LEV, LAT, LON), ((1, 8),), -0.2, 0.2)), 0.25, 1.0)
    return {"perturb": perturb, "gradient": gradient, "k_north": k_north, "k_east": k_east, "scale": scale}


def spread(values, k_north, k_east):
    middle = values[..., 1:-1, :]
    north_flux = k_north[:, 1:-1] * (values[..., 2:, :] - middle)
    south_flux = k_north[:, :-2] * (middle - values[..., :-2, :])
    east_face = k_east[:, 1:-1]
    east_flux = east_face * (jnp.roll(middle, -1, -1) - middle) - jnp.roll(east_face, 1, -1) * (middle - jnp.roll(middle, 1, -1))
    return north_flux - south_flux + east_flux


def pad_rows(array):
    widths = [(0, 0)] * (array.ndim - 2) + [(1, 1), (0, 0)]
    return jnp.pad(array, widths)


def reference(perturb, gradient, k_north, k_east, scale):
    row_total = k_north.shape[1]
    top_row = jnp.arange(row_total) == row_total - 1
    masked_north = jnp.where(top_row[None, :, None], jnp.float32(0.0), k_north)
    padded_north = pad_rows(masked_north)
    padded_east = pad_rows(k_east)
    padded_scale = pad_rows(scale)

    def member_block(running, block_data):
        member_data = block_data.astype(jnp.float32)
        field = member_data * gradient[None]
        for repeat in range(SWEEP):
            field = field + spread(pad_rows(field) * padded_scale, padded_north, padded_east)
        for repeat in range(SWEEP):
            field = field + scale * spread(pad_rows(field), padded_north, padded_east)
        return running + jnp.sum(member_data * field, axis=0), None

    blocks = perturb.reshape(N_MEM, MEM_DEV, perturb.shape[1], perturb.shape[2], perturb.shape[3])
    start_sum = jnp.zeros(gradient.shape, jnp.float32)
    running, unused = lax.scan(member_block, start_sum, blocks)
    return running / jnp.float32(MEM_DEV * N_MEM - 1)
```

```python
import jax
import jax.numpy as jnp
from jax import lax
from jax.experimental import pallas as pl
from jax.experimental.pallas import tpu as pltpu
from jax.sharding import Mesh
from jax.sharding import PartitionSpec as P

SWEEP = 4
MEM = ("mem_0", "mem_1", "mem_2")
CHIP = ("mem_0", "mem_1")
HALO = 2 * SWEEP
GROUP = 32
LANES = 128


def regroup(tiles, lane):
    result = []
    for j in range(4):
        value = None
        for l in range(4):
            moved = tiles[l] if l == j else pltpu.roll(tiles[l], ((l - j) * GROUP) % LANES, 1)
            value = moved if value is None else jnp.where(lane < l * GROUP, value, moved)
        result.append(value)
    return result


def kernel(flags, perturb, k_north, k_east, scale, low, high, mine, other,
           keep, send, field, member, north, east, step, inverse, total):
    levels, rows, width = k_north.shape
    span = rows + 2 * HALO
    tiles = width // LANES
    core = flags[0]
    is_top = flags[1]

    row = lax.broadcasted_iota(jnp.int32, (rows, LANES), 0)
    edge = (row == rows - 1) & (is_top == 1)
    for t in range(tiles):
        cols = slice(t * LANES, (t + 1) * LANES)
        for l in range(levels):
            for m in range(4):
                at = (m // 2) * 8 + 2 * l + m % 2
                member[t, pl.ds(at, HALO, stride=16), :] = low[4 * m + l, :, cols]
                member[t, pl.ds(HALO * 16 + at, rows, stride=16), :] = perturb[
                    m, l, :, cols
                ].astype(jnp.float32)
                member[t, pl.ds((HALO + rows) * 16 + at, HALO, stride=16), :] = high[
                    4 * m + l, :, cols
                ]
            masked = jnp.where(edge, 0.0, k_north[l, :, cols])
            middles = ((north, masked), (east, k_east[l, :, cols]), (step, scale[l, :, cols]))
            for a, (ref, middle) in enumerate(middles):
                for twin in range(2):
                    at = 2 * l + twin
                    ref[t, pl.ds(at, HALO, stride=8), :] = low[16 + 4 * a + l, :, cols]
                    ref[t, pl.ds(HALO * 8 + at, rows, stride=8), :] = middle
                    ref[t, pl.ds((HALO + rows) * 8 + at, HALO, stride=8), :] = high[
                        16 + 4 * a + l, :, cols
                    ]

    lane = lax.broadcasted_iota(jnp.int32, (span, LANES), 1)
    for t in range(tiles):
        blocks = []
        for j in range(4):
            chip, owner = 2 * t + j // 2, j % 2
            blocks.append(jnp.where(core == owner, mine[chip], other[chip]))
        for l, value in enumerate(regroup(blocks, lane)):
            for twin in range(2):
                inverse[t, pl.ds(2 * l + twin, span, stride=8), :] = value

    def at8(j):
        return pl.ds(pl.multiple_of(j * 8, 8), 8)

    def at16(j, pair):
        return pl.ds(pl.multiple_of(j * 16 + 8 * pair, 8), 8)

    def start(j, _):
        for t in range(tiles):
            s = step[t, at8(j), :]
            sg = s * inverse[t, at8(j), :]
            for pair in range(2):
                field[t, at16(j, pair), :] = member[t, at16(j, pair), :] * sg
            inverse[t, at8(j), :] = 1.0 / jnp.where(s == 0.0, 1.0, s)
        return 0

    lax.fori_loop(0, span, start, 0)

    lane = lax.broadcasted_iota(jnp.int32, (8, LANES), 1)

    def shifted(values, amount):
        moved = [pltpu.roll(v, amount % LANES, 1) for v in values]
        edge = lane == (LANES - 1 if amount < 0 else 0)
        return [jnp.where(edge, moved[(t - amount) % tiles], moved[t]) for t in range(tiles)]

    def sweep(first, last, finish):
        for pair in range(2):
            def load(j):
                return [field[t, at16(j, pair), :] for t in range(tiles)]

            def one(j, carry):
                here, south = carry
                above = load(j + 1)
                flux = [north[t, at8(j), :] * (above[t] - here[t]) for t in range(tiles)]
                ahead = shifted(here, -1)
                side = [east[t, at8(j), :] * (ahead[t] - here[t]) for t in range(tiles)]
                behind = shifted(side, 1)
                for t in range(tiles):
                    change = (flux[t] - south[t]) + (side[t] - behind[t])
                    value = here[t] + step[t, at8(j), :] * change
                    if finish:
                        value = value * inverse[t, at8(j), :]
                    field[t, at16(j, pair), :] = value
                return above, flux

            here, before = load(first), load(first - 1)
            south = [north[t, at8(first - 1), :] * (here[t] - before[t]) for t in range(tiles)]
            lax.fori_loop(first, last, one, (here, south))

    for n in range(2 * SWEEP):
        sweep(n + 1, span - n - 1, n == SWEEP - 1)

    def gather(j, _):
        for t in range(tiles):
            value = None
            for pair in range(2):
                term = member[t, at16(j + HALO, pair), :] * field[t, at16(j + HALO, pair), :]
                value = term if value is None else value + term
            total[t, at8(j), :] = value
        return 0

    lax.fori_loop(0, rows, gather, 0)

    lane = lax.broadcasted_iota(jnp.int32, (rows, LANES), 1)
    for t in range(tiles):
        sums = [
            total[t, pl.ds(2 * l, rows, stride=8), :] + total[t, pl.ds(2 * l + 1, rows, stride=8), :]
            for l in range(levels)
        ]
        blocks = regroup(sums, lane)
        for k in range(2):
            a, b = blocks[2 * k], blocks[2 * k + 1]
            keep[2 * t + k] = jnp.where(core == 0, a, b)
            send[2 * t + k] = jnp.where(core == 0, b, a)


def shards(perturb, gradient, k_north, k_east, scale):
    members, levels, rows, width = perturb.shape
    span = rows + 2 * HALO
    size = lax.axis_size("lat")
    up = [(i, i + 1) for i in range(size - 1)]
    down = [(j, i) for i, j in up]
    swap = [(0, 1), (1, 0)]
    core = lax.axis_index("mem_2")
    is_top = (lax.axis_index("lat") == size - 1).astype(jnp.int32)
    flags = jnp.stack([core.astype(jnp.int32), is_top])

    packed = gradient.transpose(1, 0, 2).reshape(rows, levels * GROUP)
    below = lax.ppermute(packed[rows - HALO:], "lat", up)
    above = lax.ppermute(packed[:HALO], "lat", down)

    def edge(start):
        parts = [perturb[:, :, start:start + HALO].astype(jnp.float32).reshape(-1, HALO, width)]
        parts += [a[:, start:start + HALO] for a in (k_north, k_east, scale)]
        return jnp.concatenate(parts, axis=0)

    low = lax.ppermute(edge(rows - HALO), "lat", up)
    high = lax.ppermute(edge(0), "lat", down)

    chips = lax.axis_size(CHIP)
    block = jnp.concatenate([below, packed, above], axis=0)
    mine = lax.all_to_all(
        jnp.broadcast_to(block[None], (chips, span, LANES)), CHIP, 0, 0, tiled=True
    )
    other = lax.ppermute(mine, "mem_2", swap)

    vmem = pl.BlockSpec(memory_space=pltpu.VMEM)
    part = jax.ShapeDtypeStruct((chips, rows, LANES), jnp.float32)
    keep, send = pl.pallas_call(
        kernel,
        out_shape=(part, part),
        in_specs=[pl.BlockSpec(memory_space=pltpu.SMEM)] + [vmem] * 8,
        out_specs=(vmem, vmem),
        scratch_shapes=[
            pltpu.VMEM((width // LANES, span * 16, LANES), jnp.float32),
            pltpu.VMEM((width // LANES, span * 16, LANES), jnp.float32),
            pltpu.VMEM((width // LANES, span * 8, LANES), jnp.float32),
            pltpu.VMEM((width // LANES, span * 8, LANES), jnp.float32),
            pltpu.VMEM((width // LANES, span * 8, LANES), jnp.float32),
            pltpu.VMEM((width // LANES, span * 8, LANES), jnp.float32),
            pltpu.VMEM((width // LANES, rows * 8, LANES), jnp.float32),
        ],
        compiler_params=pltpu.CompilerParams(vmem_limit_bytes=40 * 2**20),
        name="diffuse",
    )(flags, perturb, k_north, k_east, scale, low, high, mine, other)

    merged = keep + lax.ppermute(send, "mem_2", swap)
    parts = lax.all_to_all(merged, CHIP, 0, 0, tiled=True)
    total = jnp.sum(parts, axis=0) / jnp.float32(members * lax.axis_size(MEM) - 1)
    return total.reshape(rows, levels, GROUP).transpose(1, 0, 2)


def solution(mesh):
    torus = Mesh(
        mesh.devices.reshape(4, 4, 2, mesh.shape["lat"]), ("mem_0", "mem_1", "mem_2", "lat")
    )
    in_specs = (
        P(MEM, None, "lat", None),
        P(None, "lat", MEM),
        P(None, "lat", None),
        P(None, "lat", None),
        P(None, "lat", None),
    )
    out_specs = P(None, "lat", MEM)
    return jax.shard_map(
        shards, mesh=torus, in_specs=in_specs, out_specs=out_specs, check_vma=False
    )
```

```python
import jax
import jax.numpy as jnp
from jax import lax
from jax.experimental import pallas as pl
from jax.experimental.pallas import tpu as pltpu
from jax.sharding import Mesh
from jax.sharding import PartitionSpec as P

SWEEP = 4
MEM = ("mem_0", "mem_1", "mem_2")
CHIP = ("mem_0", "mem_1")
HALO = 2 * SWEEP
GROUP = 32
LANES = 128
UNROLL = 4
F32 = jnp.float32
BF16 = jnp.bfloat16


def splitting(length, period):
    source = lax.broadcasted_iota(jnp.int32, (length, length), 0)
    target = lax.broadcasted_iota(jnp.int32, (length, length), 1)
    return one_hot(source, target, period)


def one_hot(source, target, period):
    inner = source & (period - 1)
    moved = (source - inner) + (inner & 1) * (period // 2) + (inner >> 1)
    return (moved == target).astype(F32).astype(BF16)


def exact_dot(values, matrix):
    high = values.astype(BF16)
    rest = values - high.astype(F32)
    mid = rest.astype(BF16)
    low = (rest - mid.astype(F32)).astype(BF16)

    def dot(part):
        return jnp.dot(part, matrix, preferred_element_type=F32)

    return (dot(high) + dot(mid)) + dot(low)


def exchange(values, lane):
    values = list(values)
    width = LANES // 8
    for d in (1, 2, 4):
        is_set = (lane & (width * d)) != 0
        for i in range(8):
            if i & d:
                continue
            a, b = values[i], values[i + d]
            values[i] = jnp.where(is_set, pltpu.roll(b, width * d, 1), a)
            values[i + d] = jnp.where(is_set, b, pltpu.roll(a, LANES - width * d, 1))
    return values


def at8(j):
    return pl.ds(pl.multiple_of(j * 8, 8), 8)


def at16(j, pair):
    return pl.ds(pl.multiple_of(j * 16 + 8 * pair, 8), 8)


def neighbours(values, lane):
    even, odd = values[:4], values[4:]
    east = [pltpu.roll(v, LANES - 1, 1) for v in even]
    west = [pltpu.roll(v, 1, 1) for v in odd]
    east = [jnp.where(lane == LANES - 1, east[(t + 1) % 4], east[t]) for t in range(4)]
    west = [jnp.where(lane == 0, west[(t - 1) % 4], west[t]) for t in range(4)]
    return odd + east, west + even


def pack_kernel(gradient, packed):
    joined = jnp.concatenate([gradient[l] for l in range(gradient.shape[0])], axis=1)
    packed[...] = exact_dot(joined, splitting(LANES, GROUP))


def edge_kernel(perturb, k_north, k_east, scale, out):
    for m in range(4):
        for l in range(4):
            out[4 * m + l] = perturb[m, l].astype(F32)
    for a, ref in enumerate((k_north, k_east, scale)):
        for l in range(4):
            out[16 + 4 * a + l] = ref[l]


def finish_kernel(count, parts, out):
    total = parts[0]
    for k in range(1, parts.shape[0]):
        total = total + parts[k]
    total = total / F32(count)
    source = lax.broadcasted_iota(jnp.int32, (LANES, LANES), 1)
    target = lax.broadcasted_iota(jnp.int32, (LANES, LANES), 0)
    total = exact_dot(total, one_hot(source, target, GROUP))
    for l in range(out.shape[0]):
        out[l] = total[:, l * GROUP:(l + 1) * GROUP]


def coefficients(rows, refs, lane):
    north, east, step, to_north, to_south, to_east, to_west, centre, inverse = refs

    def one(j):
        s = [step[t, at8(j), :] for t in range(8)]
        e = [east[t, at8(j), :] for t in range(8)]
        _, w = neighbours(e, lane)
        for t in range(8):
            up = s[t] * north[t, at8(j), :]
            down = s[t] * north[t, at8(j - 1), :]
            right = s[t] * e[t]
            left = s[t] * w[t]
            to_north[t, at8(j), :] = up
            to_south[t, at8(j), :] = down
            to_east[t, at8(j), :] = right
            to_west[t, at8(j), :] = left
            centre[t, at8(j), :] = 1.0 - ((up + down) + (right + left))
            inverse[t, at8(j), :] = 1.0 / jnp.where(s[t] == 0.0, 1.0, s[t])

    first, last = rows
    lax.fori_loop(first, last, lambda j, _: (one(j), 0)[1], 0)


def prepare_kernel(flags, perturb, k_north, k_east, scale, member, *refs):
    levels, rows, width = k_north.shape
    north, east, step = refs[:3]
    matrix = splitting(256, 256)
    row = lax.broadcasted_iota(jnp.int32, (rows, 256), 0)
    edge = (row == rows - 1) & (flags[1] == 1)
    for u in range(width // 256):
        cols = slice(u * 256, (u + 1) * 256)
        for m in range(4):
            values = jnp.dot(
                perturb[m, :, :, cols].reshape(levels * rows, 256), matrix,
                preferred_element_type=F32,
            )
            for l in range(levels):
                at = HALO * 16 + (m // 2) * 8 + 2 * l + m % 2
                for odd in range(2):
                    member[u + 4 * odd, pl.ds(at, rows, stride=16), :] = values[
                        l * rows:(l + 1) * rows, odd * LANES:(odd + 1) * LANES
                    ]
        for ref, source in ((north, k_north), (east, k_east), (step, scale)):
            parts = [source[l, :, cols] for l in range(levels)]
            if ref is north:
                parts = [jnp.where(edge, 0.0, part) for part in parts]
            values = exact_dot(jnp.concatenate(parts, axis=0), matrix)
            for l in range(levels):
                for odd in range(2):
                    value = values[l * rows:(l + 1) * rows, odd * LANES:(odd + 1) * LANES]
                    for twin in range(2):
                        at = HALO * 8 + 2 * l + twin
                        ref[u + 4 * odd, pl.ds(at, rows, stride=8), :] = value
    lane = lax.broadcasted_iota(jnp.int32, (8, LANES), 1)
    coefficients((HALO + 1, HALO + rows), refs, lane)


def sweep_kernel(flags, low, high, mine, other, *args):
    keep, send = args[10:12]
    member, *refs = args[12:22]
    scratch = args[22:]
    step, (to_north, to_south, to_east, to_west, centre, inverse) = refs[2], refs[3:]
    fields, guess, total = scratch[:2], scratch[2], scratch[3]
    rows, levels, span = keep.shape[1], 4, mine.shape[1]
    core = flags[0]
    matrix = splitting(256, 256)
    lane = lax.broadcasted_iota(jnp.int32, (8, LANES), 1)

    for u in range(low.shape[2] // 256):
        cols = slice(u * 256, (u + 1) * 256)
        for source, first in ((low, 0), (high, HALO + rows)):
            values = jnp.dot(
                source[:16, :, cols].reshape(16 * HALO, 256).astype(BF16), matrix,
                preferred_element_type=F32,
            )
            for m in range(4):
                for l in range(levels):
                    at = first * 16 + (m // 2) * 8 + 2 * l + m % 2
                    k = (m * levels + l) * HALO
                    for odd in range(2):
                        member[u + 4 * odd, pl.ds(at, HALO, stride=16), :] = values[
                            k:k + HALO, odd * LANES:(odd + 1) * LANES
                        ]
            values = exact_dot(source[16:, :, cols].reshape(12 * HALO, 256), matrix)
            for a in range(3):
                for l in range(levels):
                    k = (a * levels + l) * HALO
                    for odd in range(2):
                        for twin in range(2):
                            at = first * 8 + 2 * l + twin
                            refs[a][u + 4 * odd, pl.ds(at, HALO, stride=8), :] = values[
                                k:k + HALO, odd * LANES:(odd + 1) * LANES
                            ]
    for t in range(8):
        last = (t, at8(HALO - 1), slice(None))
        refs[0][last] = jnp.where(flags[2] == 1, 0.0, refs[0][last])
    coefficients((1, HALO + 1), refs, lane)
    coefficients((HALO + rows, span), refs, lane)

    wide = lax.broadcasted_iota(jnp.int32, (span, LANES), 1)
    for u in range(4):
        blocks = []
        for k in range(8):
            chip, owner = 4 * u + k // 2, k % 2
            blocks.append(jnp.where(core == owner, mine[chip], other[chip]))
        for k, value in enumerate(exchange(blocks, wide)):
            l, odd = k // 2, k % 2
            for twin in range(2):
                guess[u + 4 * odd, pl.ds(2 * l + twin, span, stride=8), :] = value

    def start(j, _):
        for t in range(8):
            scaled = step[t, at8(j), :] * guess[t, at8(j), :]
            for pair in range(2):
                fields[0][t, at16(j, pair), :] = member[t, at16(j, pair), :] * scaled
        return 0

    lax.fori_loop(0, span, start, 0)

    def advance(source, target, first, count, finish):
        def chunk(i, _):
            for k in range(UNROLL):
                j = first + i * UNROLL + k
                for pair in range(2):
                    here = [source[t, at16(j, pair), :] for t in range(8)]
                    right, left = neighbours(here, lane)
                    for t in range(8):
                        value = centre[t, at8(j), :] * here[t]
                        value += to_north[t, at8(j), :] * source[t, at16(j + 1, pair), :]
                        value += to_south[t, at8(j), :] * source[t, at16(j - 1, pair), :]
                        side = to_east[t, at8(j), :] * right[t] + to_west[t, at8(j), :] * left[t]
                        value += side
                        if finish:
                            value = value * inverse[t, at8(j), :]
                        target[t, at16(j, pair), :] = value
            return 0

        lax.fori_loop(0, -(-count // UNROLL), chunk, 0)

    for n in range(2 * SWEEP):
        advance(fields[n % 2], fields[1 - n % 2], n + 1, span - 2 * n - 2, n == SWEEP - 1)
    result = fields[0]

    def gather(j, _):
        for t in range(8):
            value = None
            for pair in range(2):
                term = member[t, at16(j + HALO, pair), :] * result[t, at16(j + HALO, pair), :]
                value = term if value is None else value + term
            total[t, at8(j), :] = value
        return 0

    lax.fori_loop(0, rows, gather, 0)

    wide = lax.broadcasted_iota(jnp.int32, (rows, LANES), 1)
    for u in range(4):
        sums = []
        for k in range(8):
            l, t = k // 2, u + 4 * (k % 2)
            sums.append(
                total[t, pl.ds(2 * l, rows, stride=8), :]
                + total[t, pl.ds(2 * l + 1, rows, stride=8), :]
            )
        blocks = exchange(sums, wide)
        for k in range(4):
            a, b = blocks[2 * k], blocks[2 * k + 1]
            keep[4 * u + k] = jnp.where(core == 0, a, b)
            send[4 * u + k] = jnp.where(core == 0, b, a)


def shards(perturb, gradient, k_north, k_east, scale):
    members, levels, rows, width = perturb.shape
    span = rows + 2 * HALO
    size = lax.axis_size("lat")
    up = [(i, (i + 1) % size) for i in range(size)]
    down = [(j, i) for i, j in up]
    swap = [(0, 1), (1, 0)]
    core = lax.axis_index("mem_2")
    place = lax.axis_index("lat")
    flags = jnp.stack([core, place == size - 1, place == 0]).astype(jnp.int32)
    vmem = pl.BlockSpec(memory_space=pltpu.VMEM)
    smem = pl.BlockSpec(memory_space=pltpu.SMEM)

    packed = pl.pallas_call(
        pack_kernel,
        out_shape=jax.ShapeDtypeStruct((rows, LANES), F32),
        in_specs=[vmem], out_specs=vmem, name="pack",
    )(gradient)
    below = lax.ppermute(packed[rows - HALO:], "lat", up)
    above = lax.ppermute(packed[:HALO], "lat", down)

    def edge(block):
        short = pl.BlockSpec((levels, HALO, width), lambda i: (0, block, 0))
        return pl.pallas_call(
            edge_kernel,
            out_shape=jax.ShapeDtypeStruct((7 * levels, HALO, width), F32),
            grid=(1,),
            in_specs=[pl.BlockSpec((4, levels, HALO, width), lambda i: (0, 0, block, 0))] + [short] * 3,
            out_specs=pl.BlockSpec((7 * levels, HALO, width), lambda i: (0, 0, 0)),
            compiler_params=pltpu.CompilerParams(vmem_limit_bytes=8 * 2**20),
            cost_estimate=pl.CostEstimate(flops=0, bytes_accessed=2 * 2**20, transcendentals=0),
            name="edges",
        )(perturb, k_north, k_east, scale)

    top, bottom = edge(rows // HALO - 1), edge(0)
    low = lax.ppermute(top, "lat", up)
    high = lax.ppermute(bottom, "lat", down)

    chips = lax.axis_size(CHIP)
    block = jnp.concatenate([below, packed, above], axis=0)
    spread = jnp.broadcast_to(block[None], (chips, span, LANES))
    mine = lax.all_to_all(spread, CHIP, 0, 0, tiled=True)
    other = lax.ppermute(mine, "mem_2", swap)

    padded = span + UNROLL
    tall = pltpu.VMEM((8, padded * 16, LANES), F32)
    short = pltpu.VMEM((8, padded * 8, LANES), F32)
    prepare = pl.pallas_call(
        prepare_kernel,
        out_shape=[tall] + [short] * 9,
        in_specs=[smem] + [vmem] * 4,
        out_specs=[vmem] * 10,
        compiler_params=pltpu.CompilerParams(vmem_limit_bytes=8 * 2**20),
        cost_estimate=pl.CostEstimate(flops=0, bytes_accessed=24 * 2**20, transcendentals=0),
        name="prepare",
    )
    prepared = prepare(flags, perturb, k_north, k_east, scale)

    part = jax.ShapeDtypeStruct((chips, rows, LANES), F32)
    keep, send = pl.pallas_call(
        sweep_kernel,
        out_shape=[part, part] + [tall] + [short] * 9,
        in_specs=[smem] + [vmem] * 14,
        out_specs=[vmem] * 12,
        input_output_aliases={5 + k: 2 + k for k in range(10)},
        scratch_shapes=[
            tall,
            tall,
            pltpu.VMEM((8, span * 8, LANES), F32),
            pltpu.VMEM((8, rows * 8, LANES), F32),
        ],
        compiler_params=pltpu.CompilerParams(vmem_limit_bytes=18 * 2**20),
        name="sweeps",
    )(flags, low, high, mine, other, *prepared)[:2]

    merged = keep + lax.ppermute(send, "mem_2", swap)
    parts = lax.all_to_all(merged, CHIP, 0, 0, tiled=True)
    count = members * lax.axis_size(MEM) - 1
    return pl.pallas_call(
        lambda p, o: finish_kernel(count, p, o),
        out_shape=jax.ShapeDtypeStruct((levels, rows, GROUP), F32),
        in_specs=[vmem], out_specs=vmem, name="finish",
    )(parts)


def solution(mesh):
    torus = Mesh(
        mesh.devices.reshape(4, 4, 2, mesh.shape["lat"]), ("mem_0", "mem_1", "mem_2", "lat")
    )
    in_specs = (
        P(MEM, None, "lat", None),
        P(None, "lat", MEM),
        P(None, "lat", None),
        P(None, "lat", None),
        P(None, "lat", None),
    )
    out_specs = P(None, "lat", MEM)

    return jax.shard_map(
        shards, mesh=torus, in_specs=in_specs, out_specs=out_specs, check_vma=False
    )
```

```python
import jax
import jax.numpy as jnp
from jax import lax
from jax.experimental import pallas as pl
from jax.experimental.pallas import tpu as pltpu
from jax.sharding import Mesh
from jax.sharding import PartitionSpec as P

SWEEP = 4
MEM = ("mem_0", "mem_1", "mem_2")
CHIP = ("mem_0", "mem_1")
HALO = 2 * SWEEP
GROUP = 32
LANES = 128
UNROLL = 4
CLOSED = 66_150_400
F32 = jnp.float32
BF16 = jnp.bfloat16


def splitting(length, period):
    source = lax.broadcasted_iota(jnp.int32, (length, length), 0)
    target = lax.broadcasted_iota(jnp.int32, (length, length), 1)
    return one_hot(source, target, period)


def one_hot(source, target, period):
    inner = source & (period - 1)
    moved = (source - inner) + (inner & 1) * (period // 2) + (inner >> 1)
    return (moved == target).astype(F32).astype(BF16)


def exact_dot(values, matrix):
    high = values.astype(BF16)
    rest = values - high.astype(F32)
    mid = rest.astype(BF16)
    low = (rest - mid.astype(F32)).astype(BF16)

    def dot(part):
        return jnp.dot(part, matrix, preferred_element_type=F32)

    return (dot(high) + dot(mid)) + dot(low)


def exchange(values, lane):
    values = list(values)
    width = LANES // 8
    for d in (1, 2, 4):
        is_set = (lane & (width * d)) != 0
        for i in range(8):
            if i & d:
                continue
            a, b = values[i], values[i + d]
            values[i] = jnp.where(is_set, pltpu.roll(b, width * d, 1), a)
            values[i + d] = jnp.where(is_set, b, pltpu.roll(a, LANES - width * d, 1))
    return values


def at8(j):
    return pl.ds(pl.multiple_of(j * 8, 8), 8)


def at16(j, pair):
    return pl.ds(pl.multiple_of(j * 16 + 8 * pair, 8), 8)


def neighbours(values, lane):
    even, odd = values[:4], values[4:]
    east = [pltpu.roll(v, LANES - 1, 1) for v in even]
    west = [pltpu.roll(v, 1, 1) for v in odd]
    east = [jnp.where(lane == LANES - 1, east[(t + 1) % 4], east[t]) for t in range(4)]
    west = [jnp.where(lane == 0, west[(t - 1) % 4], west[t]) for t in range(4)]
    return odd + east, west + even


def edge_kernel(gradient, perturb, k_north, k_east, scale,
                packed, first, last, top, bottom, narrow, sems):
    rows = perturb.shape[2]
    copies = []
    for side, (out, start) in enumerate(((top, rows - HALO), (bottom, 0))):
        at = pl.ds(start, HALO)
        copies.append(pltpu.make_async_copy(
            perturb.at[:, :, at, :], narrow.at[side], sems.at[side, 0]
        ))
        for a, ref in enumerate((k_north, k_east, scale)):
            copies.append(pltpu.make_async_copy(
                ref.at[:, at, :], out.at[pl.ds(16 + 4 * a, 4)], sems.at[side, 1 + a]
            ))
    for copy in copies:
        copy.start()
    joined = jnp.concatenate([gradient[l] for l in range(gradient.shape[0])], axis=1)
    value = exact_dot(joined, splitting(LANES, GROUP))
    packed[...] = value
    first[...] = value[:HALO]
    last[...] = value[-HALO:]
    for copy in copies:
        copy.wait()
    for side, out in enumerate((top, bottom)):
        for m in range(4):
            for l in range(4):
                out[4 * m + l] = narrow[side, m, l].astype(F32)


def finish_kernel(count, parts, out):
    total = parts[0]
    for k in range(1, parts.shape[0]):
        total = total + parts[k]
    total = total / F32(count)
    source = lax.broadcasted_iota(jnp.int32, (LANES, LANES), 1)
    target = lax.broadcasted_iota(jnp.int32, (LANES, LANES), 0)
    total = exact_dot(total, one_hot(source, target, GROUP))
    for l in range(out.shape[0]):
        out[l] = total[:, l * GROUP:(l + 1) * GROUP]


def coefficients(rows, refs, lane):
    north, east, step, to_north, to_south, to_east, to_west, centre, inverse = refs

    def one(j):
        s = [step[t, at8(j), :] for t in range(8)]
        e = [east[t, at8(j), :] for t in range(8)]
        _, w = neighbours(e, lane)
        for t in range(8):
            up = s[t] * north[t, at8(j), :]
            down = s[t] * north[t, at8(j - 1), :]
            right = s[t] * e[t]
            left = s[t] * w[t]
            to_north[t, at8(j), :] = up
            to_south[t, at8(j), :] = down
            to_east[t, at8(j), :] = right
            to_west[t, at8(j), :] = left
            centre[t, at8(j), :] = 1.0 - ((up + down) + (right + left))
            inverse[t, at8(j), :] = 1.0 / jnp.where(s[t] == 0.0, 1.0, s[t])

    def chunk(i, _):
        for k in range(UNROLL):
            one(rows[0] + i * UNROLL + k)
        return 0

    lax.fori_loop(0, (rows[1] - rows[0]) // UNROLL, chunk, 0)


def prepare_kernel(perturb, k_north, k_east, scale, member, *refs):
    levels, rows, width = k_north.shape
    north, east, step = refs[:3]
    matrix = splitting(256, 256)
    row = lax.broadcasted_iota(jnp.int32, (rows, 256), 0)
    edge = (row == rows - 1) & (lax.axis_index("lat") == lax.axis_size("lat") - 1)
    for u in range(width // 256):
        cols = slice(u * 256, (u + 1) * 256)
        for m in range(4):
            values = jnp.dot(
                perturb[m, :, :, cols].reshape(levels * rows, 256), matrix,
                preferred_element_type=F32,
            )
            for l in range(levels):
                at = HALO * 16 + (m // 2) * 8 + 2 * l + m % 2
                for odd in range(2):
                    member[u + 4 * odd, pl.ds(at, rows, stride=16), :] = values[
                        l * rows:(l + 1) * rows, odd * LANES:(odd + 1) * LANES
                    ]
        for ref, source in ((north, k_north), (east, k_east), (step, scale)):
            parts = [source[l, :, cols] for l in range(levels)]
            if ref is north:
                parts = [jnp.where(edge, 0.0, part) for part in parts]
            values = exact_dot(jnp.concatenate(parts, axis=0), matrix)
            for l in range(levels):
                for odd in range(2):
                    value = values[l * rows:(l + 1) * rows, odd * LANES:(odd + 1) * LANES]
                    for twin in range(2):
                        at = HALO * 8 + 2 * l + twin
                        ref[u + 4 * odd, pl.ds(at, rows, stride=8), :] = value
    lane = lax.broadcasted_iota(jnp.int32, (8, LANES), 1)
    coefficients((HALO, HALO + rows), refs, lane)


def sweep_kernel(low, high, mine, other, *args):
    keep, send = args[10:12]
    member, *refs = args[12:22]
    scratch = args[22:]
    step, (to_north, to_south, to_east, to_west, centre, inverse) = refs[2], refs[3:]
    fields, guess, total, near, sems = scratch[:2], scratch[2], scratch[3], scratch[4], scratch[5]
    rows, levels, span = keep.shape[1], 4, mine.shape[1]
    core = lax.axis_index("mem_2")
    copies = [
        pltpu.make_async_copy(source, near.at[k], sems.at[k]) for k, source in enumerate((low, high))
    ]
    for copy in copies:
        copy.start()

    wide = lax.broadcasted_iota(jnp.int32, (span, LANES), 1)
    for u in range(4):
        blocks = []
        for k in range(8):
            chip, owner = 4 * u + k // 2, k % 2
            blocks.append(jnp.where(core == owner, mine[chip], other[chip]))
        for k, value in enumerate(exchange(blocks, wide)):
            l, odd = k // 2, k % 2
            for twin in range(2):
                guess[u + 4 * odd, pl.ds(2 * l + twin, span, stride=8), :] = value

    for copy in copies:
        copy.wait()
    matrix = splitting(256, 256)
    lane = lax.broadcasted_iota(jnp.int32, (8, LANES), 1)

    for u in range(low.shape[2] // 256):
        cols = slice(u * 256, (u + 1) * 256)
        for k, first in ((0, 0), (1, HALO + rows)):
            source = near.at[k]
            values = jnp.dot(
                source[:16, :, cols].reshape(16 * HALO, 256).astype(BF16), matrix,
                preferred_element_type=F32,
            )
            for m in range(4):
                for l in range(levels):
                    at = first * 16 + (m // 2) * 8 + 2 * l + m % 2
                    at_row = (m * levels + l) * HALO
                    for odd in range(2):
                        member[u + 4 * odd, pl.ds(at, HALO, stride=16), :] = values[
                            at_row:at_row + HALO, odd * LANES:(odd + 1) * LANES
                        ]
            values = exact_dot(source[16:, :, cols].reshape(12 * HALO, 256), matrix)
            for a in range(3):
                for l in range(levels):
                    at_row = (a * levels + l) * HALO
                    for odd in range(2):
                        for twin in range(2):
                            at = first * 8 + 2 * l + twin
                            refs[a][u + 4 * odd, pl.ds(at, HALO, stride=8), :] = values[
                                at_row:at_row + HALO, odd * LANES:(odd + 1) * LANES
                            ]
    for t in range(8):
        last = (t, at8(HALO - 1), slice(None))
        refs[0][last] = jnp.where(lax.axis_index("lat") == 0, 0.0, refs[0][last])
    coefficients((1, HALO + 1), refs, lane)
    coefficients((HALO + rows, span), refs, lane)

    def start(j, _):
        for t in range(8):
            scaled = step[t, at8(j), :] * guess[t, at8(j), :]
            for pair in range(2):
                fields[0][t, at16(j, pair), :] = member[t, at16(j, pair), :] * scaled
        return 0

    lax.fori_loop(0, span, start, 0)

    def advance(source, target, first, count, finish):
        def chunk(begin, length):
            for k in range(length):
                j = begin + k
                for pair in range(2):
                    here = [source[t, at16(j, pair), :] for t in range(8)]
                    right, left = neighbours(here, lane)
                    for t in range(8):
                        value = centre[t, at8(j), :] * here[t]
                        value += to_north[t, at8(j), :] * source[t, at16(j + 1, pair), :]
                        value += to_south[t, at8(j), :] * source[t, at16(j - 1, pair), :]
                        side = to_east[t, at8(j), :] * right[t] + to_west[t, at8(j), :] * left[t]
                        value += side
                        if finish:
                            value = value * inverse[t, at8(j), :]
                        target[t, at16(j, pair), :] = value
            return 0

        count = -(-count // UNROLL) * UNROLL
        whole = count // (2 * UNROLL)
        lax.fori_loop(0, whole, lambda i, _: chunk(first + i * 2 * UNROLL, 2 * UNROLL), 0)
        if count % (2 * UNROLL):
            chunk(first + whole * 2 * UNROLL, UNROLL)

    for n in range(2 * SWEEP):
        advance(fields[n % 2], fields[1 - n % 2], n + 1, span - 2 * n - 2, n == SWEEP - 1)
    result = fields[0]

    def gather(j, _):
        for t in range(8):
            value = None
            for pair in range(2):
                term = member[t, at16(j + HALO, pair), :] * result[t, at16(j + HALO, pair), :]
                value = term if value is None else value + term
            total[t, at8(j), :] = value
        return 0

    lax.fori_loop(0, rows, gather, 0)

    wide = lax.broadcasted_iota(jnp.int32, (rows, LANES), 1)
    for u in range(4):
        sums = []
        for k in range(8):
            l, t = k // 2, u + 4 * (k % 2)
            sums.append(
                total[t, pl.ds(2 * l, rows, stride=8), :]
                + total[t, pl.ds(2 * l + 1, rows, stride=8), :]
            )
        blocks = exchange(sums, wide)
        for k in range(4):
            a, b = blocks[2 * k], blocks[2 * k + 1]
            keep[4 * u + k] = jnp.where(core == 0, a, b)
            send[4 * u + k] = jnp.where(core == 0, b, a)


def shards(perturb, gradient, k_north, k_east, scale):
    members, levels, rows, width = perturb.shape
    span = rows + 2 * HALO
    size = lax.axis_size("lat")
    up = [(i, (i + 1) % size) for i in range(size)]
    down = [(j, i) for i, j in up]
    swap = [(0, 1), (1, 0)]
    vmem = pl.BlockSpec(memory_space=pltpu.VMEM)
    hbm = pl.BlockSpec(memory_space=pltpu.HBM)

    rim = jax.ShapeDtypeStruct((HALO, LANES), F32)
    edges = jax.ShapeDtypeStruct((7 * levels, HALO, width), F32)
    packed, first, last, top, bottom = pl.pallas_call(
        edge_kernel,
        out_shape=[jax.ShapeDtypeStruct((rows, LANES), F32), rim, rim, edges, edges],
        in_specs=[vmem] + [hbm] * 4, out_specs=[vmem] * 5,
        scratch_shapes=[
            pltpu.VMEM((2, 4, levels, HALO, width), BF16), pltpu.SemaphoreType.DMA((2, 4)),
        ],
        compiler_params=pltpu.CompilerParams(vmem_limit_bytes=CLOSED),
        name="edges",
    )(gradient, perturb, k_north, k_east, scale)
    below = lax.ppermute(last, "lat", up)
    above = lax.ppermute(first, "lat", down)
    low = lax.ppermute(top, "lat", up)
    high = lax.ppermute(bottom, "lat", down)

    chips = lax.axis_size(CHIP)
    block = jnp.concatenate([below, packed, above], axis=0)
    spread = jnp.broadcast_to(block[None], (chips, span, LANES))
    mine = lax.all_to_all(spread, CHIP, 0, 0, tiled=True)
    other = lax.ppermute(mine, "mem_2", swap)

    padded = span + UNROLL
    tall = pltpu.VMEM((8, padded * 16, LANES), F32)
    short = pltpu.VMEM((8, padded * 8, LANES), F32)
    prepare = pl.pallas_call(
        prepare_kernel,
        out_shape=[tall] + [short] * 9,
        in_specs=[vmem] * 4,
        out_specs=[vmem] * 10,
        compiler_params=pltpu.CompilerParams(vmem_limit_bytes=44 * 2**20),
        cost_estimate=pl.CostEstimate(flops=0, bytes_accessed=24 * 2**20, transcendentals=0),
        name="prepare",
    )
    prepared = prepare(perturb, k_north, k_east, scale)

    part = jax.ShapeDtypeStruct((chips, rows, LANES), F32)
    keep, send = pl.pallas_call(
        sweep_kernel,
        out_shape=[part, part] + [tall] + [short] * 9,
        in_specs=[hbm] * 2 + [vmem] * 12,
        out_specs=[vmem] * 12,
        input_output_aliases={4 + k: 2 + k for k in range(10)},
        scratch_shapes=[
            tall,
            tall,
            pltpu.VMEM((8, span * 8, LANES), F32),
            pltpu.VMEM((8, rows * 8, LANES), F32),
            pltpu.VMEM((2, 7 * levels, HALO, width), F32),
            pltpu.SemaphoreType.DMA((2,)),
        ],
        compiler_params=pltpu.CompilerParams(vmem_limit_bytes=18 * 2**20),
        name="sweeps",
    )(low, high, mine, other, *prepared)[:2]

    merged = keep + lax.ppermute(send, "mem_2", swap)
    parts = lax.all_to_all(merged, CHIP, 0, 0, tiled=True)
    count = members * lax.axis_size(MEM) - 1
    return pl.pallas_call(
        lambda p, o: finish_kernel(count, p, o),
        out_shape=jax.ShapeDtypeStruct((levels, rows, GROUP), F32),
        in_specs=[vmem], out_specs=vmem,
        compiler_params=pltpu.CompilerParams(vmem_limit_bytes=4 * 2**20),
        name="finish",
    )(parts)


def solution(mesh):
    torus = Mesh(
        mesh.devices.reshape(4, 4, 2, mesh.shape["lat"]), ("mem_0", "mem_1", "mem_2", "lat")
    )
    in_specs = (
        P(MEM, None, "lat", None),
        P(None, "lat", MEM),
        P(None, "lat", None),
        P(None, "lat", None),
        P(None, "lat", None),
    )
    out_specs = P(None, "lat", MEM)

    return jax.shard_map(
        shards, mesh=torus, in_specs=in_specs, out_specs=out_specs, check_vma=False
    )
```

```python
import jax
import jax.numpy as jnp
from jax import lax
from jax.experimental import pallas as pl
from jax.experimental.pallas import tpu as pltpu
from jax.sharding import Mesh
from jax.sharding import PartitionSpec as P

SWEEP = 4
MEM = ("mem_0", "mem_1", "mem_2")
CHIP = ("mem_0", "mem_1")
HALO = 2 * SWEEP
GROUP = 32
LANES = 128
UNROLL = 4
CLOSED = 66_150_400
F32 = jnp.float32
BF16 = jnp.bfloat16


def splitting(length, period):
    source = lax.broadcasted_iota(jnp.int32, (length, length), 0)
    target = lax.broadcasted_iota(jnp.int32, (length, length), 1)
    return one_hot(source, target, period)


def one_hot(source, target, period):
    inner = source & (period - 1)
    moved = (source - inner) + (inner & 1) * (period // 2) + (inner >> 1)
    return (moved == target).astype(F32).astype(BF16)


def exact_dot(values, matrix):
    high = values.astype(BF16)
    rest = values - high.astype(F32)
    mid = rest.astype(BF16)
    low = (rest - mid.astype(F32)).astype(BF16)

    def dot(part):
        return jnp.dot(part, matrix, preferred_element_type=F32)

    return (dot(high) + dot(mid)) + dot(low)


def exchange(values, lane):
    values = list(values)
    width = LANES // 8
    for d in (1, 2, 4):
        is_set = (lane & (width * d)) != 0
        for i in range(8):
            if i & d:
                continue
            a, b = values[i], values[i + d]
            values[i] = jnp.where(is_set, pltpu.roll(b, width * d, 1), a)
            values[i + d] = jnp.where(is_set, b, pltpu.roll(a, LANES - width * d, 1))
    return values


def at8(j):
    return pl.ds(pl.multiple_of(j * 8, 8), 8)


def at16(j, pair):
    return pl.ds(pl.multiple_of(j * 16 + 8 * pair, 8), 8)


def neighbours(values, lane):
    even, odd = values[:4], values[4:]
    east = [pltpu.roll(v, LANES - 1, 1) for v in even]
    west = [pltpu.roll(v, 1, 1) for v in odd]
    east = [jnp.where(lane == LANES - 1, east[(t + 1) % 4], east[t]) for t in range(4)]
    west = [jnp.where(lane == 0, west[(t - 1) % 4], west[t]) for t in range(4)]
    return odd + east, west + even


def edge_kernel(gradient, perturb, k_north, k_east, scale, packed, first, last, top, bottom,
                block, narrow, wide, arrive, leave):
    rows = perturb.shape[2]
    load = pltpu.make_async_copy(gradient, block, arrive.at[2, 0])
    load.start()
    inward, outward = [], []
    for side, (out, start) in enumerate(((top, rows - HALO), (bottom, 0))):
        at = pl.ds(start, HALO)
        inward.append([
            pltpu.make_async_copy(ref.at[:, at, :], wide.at[side, pl.ds(16 + 4 * a, 4)],
                                  arrive.at[side, a])
            for a, ref in enumerate((k_north, k_east, scale))
        ] + [pltpu.make_async_copy(perturb.at[:, :, at, :], narrow.at[side], arrive.at[side, 3])])
        outward.append([
            pltpu.make_async_copy(wide.at[side, pl.ds(k, 4)], out.at[pl.ds(k, 4)],
                                  leave.at[side, k // 4])
            for k in range(0, 28, 4)
        ])
    for side in range(2):
        for copy in inward[side]:
            copy.start()
    load.wait()
    joined = jnp.concatenate([block[l] for l in range(block.shape[0])], axis=1)
    value = exact_dot(joined, splitting(LANES, GROUP))
    packed[...] = value
    first[...] = value[:HALO]
    last[...] = value[-HALO:]
    for side in range(2):
        for a in range(3):
            inward[side][a].wait()
            outward[side][4 + a].start()
    for side in range(2):
        inward[side][3].wait()
        for m in range(4):
            for l in range(4):
                wide[side, 4 * m + l] = narrow[side, m, l].astype(F32)
            outward[side][m].start()
    for side in range(2):
        for copy in outward[side]:
            copy.wait()


def finish_kernel(count, parts, out):
    total = parts[0]
    for k in range(1, parts.shape[0]):
        total = total + parts[k]
    total = total / F32(count)
    source = lax.broadcasted_iota(jnp.int32, (LANES, LANES), 1)
    target = lax.broadcasted_iota(jnp.int32, (LANES, LANES), 0)
    total = exact_dot(total, one_hot(source, target, GROUP))
    for l in range(out.shape[0]):
        out[l] = total[:, l * GROUP:(l + 1) * GROUP]


def coefficients(rows, refs, lane):
    north, east, step, to_north, to_south, to_east, to_west, centre, inverse = refs

    def one(j):
        s = [step[t, at8(j), :] for t in range(8)]
        e = [east[t, at8(j), :] for t in range(8)]
        _, w = neighbours(e, lane)
        for t in range(8):
            up = s[t] * north[t, at8(j), :]
            down = s[t] * north[t, at8(j - 1), :]
            right = s[t] * e[t]
            left = s[t] * w[t]
            to_north[t, at8(j), :] = up
            to_south[t, at8(j), :] = down
            to_east[t, at8(j), :] = right
            to_west[t, at8(j), :] = left
            centre[t, at8(j), :] = 1.0 - ((up + down) + (right + left))
            inverse[t, at8(j), :] = 1.0 / jnp.where(s[t] == 0.0, 1.0, s[t])

    def chunk(i, _):
        for k in range(UNROLL):
            one(rows[0] + i * UNROLL + k)
        return 0

    lax.fori_loop(0, (rows[1] - rows[0]) // UNROLL, chunk, 0)


def prepare_kernel(perturb, k_north, k_east, scale, member, *refs):
    levels, rows, width = k_north.shape
    north, east, step = refs[:3]
    matrix = splitting(256, 256)
    row = lax.broadcasted_iota(jnp.int32, (rows, 256), 0)
    edge = (row == rows - 1) & (lax.axis_index("lat") == lax.axis_size("lat") - 1)
    for u in range(width // 256):
        cols = slice(u * 256, (u + 1) * 256)
        for m in range(4):
            values = jnp.dot(
                perturb[m, :, :, cols].reshape(levels * rows, 256), matrix,
                preferred_element_type=F32,
            )
            for l in range(levels):
                at = HALO * 16 + (m // 2) * 8 + 2 * l + m % 2
                for odd in range(2):
                    member[u + 4 * odd, pl.ds(at, rows, stride=16), :] = values[
                        l * rows:(l + 1) * rows, odd * LANES:(odd + 1) * LANES
                    ]
        for ref, source in ((north, k_north), (east, k_east), (step, scale)):
            parts = [source[l, :, cols] for l in range(levels)]
            if ref is north:
                parts = [jnp.where(edge, 0.0, part) for part in parts]
            values = exact_dot(jnp.concatenate(parts, axis=0), matrix)
            for l in range(levels):
                for odd in range(2):
                    value = values[l * rows:(l + 1) * rows, odd * LANES:(odd + 1) * LANES]
                    for twin in range(2):
                        at = HALO * 8 + 2 * l + twin
                        ref[u + 4 * odd, pl.ds(at, rows, stride=8), :] = value
    lane = lax.broadcasted_iota(jnp.int32, (8, LANES), 1)
    coefficients((HALO, HALO + rows), refs, lane)


def sweep_kernel(low, high, mine, other, *args):
    keep, send = args[10:12]
    member, *refs = args[12:22]
    scratch = args[22:]
    step, (to_north, to_south, to_east, to_west, centre, inverse) = refs[2], refs[3:]
    fields, guess, total, near, sems = scratch[:2], scratch[2], scratch[3], scratch[4], scratch[5]
    rows, levels, span = keep.shape[1], 4, mine.shape[1]
    core = lax.axis_index("mem_2")
    copies = [
        pltpu.make_async_copy(source, near.at[k], sems.at[k]) for k, source in enumerate((low, high))
    ]
    for copy in copies:
        copy.start()

    wide = lax.broadcasted_iota(jnp.int32, (span, LANES), 1)
    for u in range(4):
        blocks = []
        for k in range(8):
            chip, owner = 4 * u + k // 2, k % 2
            blocks.append(jnp.where(core == owner, mine[chip], other[chip]))
        for k, value in enumerate(exchange(blocks, wide)):
            l, odd = k // 2, k % 2
            for twin in range(2):
                guess[u + 4 * odd, pl.ds(2 * l + twin, span, stride=8), :] = value

    for copy in copies:
        copy.wait()
    matrix = splitting(256, 256)
    lane = lax.broadcasted_iota(jnp.int32, (8, LANES), 1)

    for u in range(low.shape[2] // 256):
        cols = slice(u * 256, (u + 1) * 256)
        for k, first in ((0, 0), (1, HALO + rows)):
            source = near.at[k]
            values = jnp.dot(
                source[:16, :, cols].reshape(16 * HALO, 256).astype(BF16), matrix,
                preferred_element_type=F32,
            )
            for m in range(4):
                for l in range(levels):
                    at = first * 16 + (m // 2) * 8 + 2 * l + m % 2
                    at_row = (m * levels + l) * HALO
                    for odd in range(2):
                        member[u + 4 * odd, pl.ds(at, HALO, stride=16), :] = values[
                            at_row:at_row + HALO, odd * LANES:(odd + 1) * LANES
                        ]
            values = exact_dot(source[16:, :, cols].reshape(12 * HALO, 256), matrix)
            for a in range(3):
                for l in range(levels):
                    at_row = (a * levels + l) * HALO
                    for odd in range(2):
                        for twin in range(2):
                            at = first * 8 + 2 * l + twin
                            refs[a][u + 4 * odd, pl.ds(at, HALO, stride=8), :] = values[
                                at_row:at_row + HALO, odd * LANES:(odd + 1) * LANES
                            ]
    for t in range(8):
        last = (t, at8(HALO - 1), slice(None))
        refs[0][last] = jnp.where(lax.axis_index("lat") == 0, 0.0, refs[0][last])
    coefficients((1, HALO + 1), refs, lane)
    coefficients((HALO + rows, span), refs, lane)

    def start(j, _):
        for t in range(8):
            scaled = step[t, at8(j), :] * guess[t, at8(j), :]
            for pair in range(2):
                fields[0][t, at16(j, pair), :] = member[t, at16(j, pair), :] * scaled
        return 0

    lax.fori_loop(0, span, start, 0)

    def advance(source, target, first, count, finish, last):
        def chunk(begin, length):
            for k in range(length):
                j = begin + k
                terms = [None] * 8
                for pair in range(2):
                    here = [source[t, at16(j, pair), :] for t in range(8)]
                    right, left = neighbours(here, lane)
                    for t in range(8):
                        value = centre[t, at8(j), :] * here[t]
                        value += to_north[t, at8(j), :] * source[t, at16(j + 1, pair), :]
                        value += to_south[t, at8(j), :] * source[t, at16(j - 1, pair), :]
                        side = to_east[t, at8(j), :] * right[t] + to_west[t, at8(j), :] * left[t]
                        value += side
                        if finish:
                            value = value * inverse[t, at8(j), :]
                        if not last:
                            target[t, at16(j, pair), :] = value
                        else:
                            term = member[t, at16(j, pair), :] * value
                            terms[t] = term if pair == 0 else terms[t] + term
                if last:
                    for t in range(8):
                        total[t, at8(j - HALO), :] = terms[t]
            return 0

        count = -(-count // UNROLL) * UNROLL
        whole = count // (2 * UNROLL)
        lax.fori_loop(0, whole, lambda i, _: chunk(first + i * 2 * UNROLL, 2 * UNROLL), 0)
        if count % (2 * UNROLL):
            chunk(first + whole * 2 * UNROLL, UNROLL)

    for n in range(2 * SWEEP):
        advance(fields[n % 2], fields[1 - n % 2], n + 1, span - 2 * n - 2,
                n == SWEEP - 1, n == 2 * SWEEP - 1)
    wide = lax.broadcasted_iota(jnp.int32, (rows, LANES), 1)
    for u in range(4):
        sums = []
        for k in range(8):
            l, t = k // 2, u + 4 * (k % 2)
            sums.append(
                total[t, pl.ds(2 * l, rows, stride=8), :]
                + total[t, pl.ds(2 * l + 1, rows, stride=8), :]
            )
        blocks = exchange(sums, wide)
        for k in range(4):
            a, b = blocks[2 * k], blocks[2 * k + 1]
            keep[4 * u + k] = jnp.where(core == 0, a, b)
            send[4 * u + k] = jnp.where(core == 0, b, a)


def shards(perturb, gradient, k_north, k_east, scale):
    members, levels, rows, width = perturb.shape
    span = rows + 2 * HALO
    size = lax.axis_size("lat")
    up = [(i, (i + 1) % size) for i in range(size)]
    down = [(j, i) for i, j in up]
    swap = [(0, 1), (1, 0)]
    vmem = pl.BlockSpec(memory_space=pltpu.VMEM)
    hbm = pl.BlockSpec(memory_space=pltpu.HBM)

    rim = jax.ShapeDtypeStruct((HALO, LANES), F32)
    edges = jax.ShapeDtypeStruct((7 * levels, HALO, width), F32)
    packed, first, last, top, bottom = pl.pallas_call(
        edge_kernel,
        out_shape=[jax.ShapeDtypeStruct((rows, LANES), F32), rim, rim, edges, edges],
        in_specs=[hbm] * 5, out_specs=[vmem] * 3 + [hbm] * 2,
        scratch_shapes=[
            pltpu.VMEM(gradient.shape, F32),
            pltpu.VMEM((2, 4, levels, HALO, width), BF16),
            pltpu.VMEM((2, 7 * levels, HALO, width), F32),
            pltpu.SemaphoreType.DMA((3, 4)),
            pltpu.SemaphoreType.DMA((2, 7)),
        ],
        compiler_params=pltpu.CompilerParams(vmem_limit_bytes=CLOSED),
        name="edges",
    )(gradient, perturb, k_north, k_east, scale)
    below = lax.ppermute(last, "lat", up)
    above = lax.ppermute(first, "lat", down)
    low = lax.ppermute(top, "lat", up)
    high = lax.ppermute(bottom, "lat", down)

    chips = lax.axis_size(CHIP)
    block = jnp.concatenate([below, packed, above], axis=0)
    spread = jnp.broadcast_to(block[None], (chips, span, LANES))
    mine = lax.all_to_all(spread, CHIP, 0, 0, tiled=True)
    other = lax.ppermute(mine, "mem_2", swap)

    padded = span + UNROLL
    tall = pltpu.VMEM((8, padded * 16, LANES), F32)
    short = pltpu.VMEM((8, padded * 8, LANES), F32)
    prepare = pl.pallas_call(
        prepare_kernel,
        out_shape=[tall] + [short] * 9,
        in_specs=[vmem] * 4,
        out_specs=[vmem] * 10,
        compiler_params=pltpu.CompilerParams(vmem_limit_bytes=44 * 2**20),
        cost_estimate=pl.CostEstimate(flops=0, bytes_accessed=24 * 2**20, transcendentals=0),
        name="prepare",
    )
    prepared = prepare(perturb, k_north, k_east, scale)

    part = jax.ShapeDtypeStruct((chips, rows, LANES), F32)
    keep, send = pl.pallas_call(
        sweep_kernel,
        out_shape=[part, part] + [tall] + [short] * 9,
        in_specs=[hbm] * 2 + [vmem] * 12,
        out_specs=[vmem] * 12,
        input_output_aliases={4 + k: 2 + k for k in range(10)},
        scratch_shapes=[
            tall,
            tall,
            pltpu.VMEM((8, span * 8, LANES), F32),
            pltpu.VMEM((8, rows * 8, LANES), F32),
            pltpu.VMEM((2, 7 * levels, HALO, width), F32),
            pltpu.SemaphoreType.DMA((2,)),
        ],
        compiler_params=pltpu.CompilerParams(vmem_limit_bytes=18 * 2**20),
        name="sweeps",
    )(low, high, mine, other, *prepared)[:2]

    merged = keep + lax.ppermute(send, "mem_2", swap)
    parts = lax.all_to_all(merged, CHIP, 0, 0, tiled=True)
    count = members * lax.axis_size(MEM) - 1
    return pl.pallas_call(
        lambda p, o: finish_kernel(count, p, o),
        out_shape=jax.ShapeDtypeStruct((levels, rows, GROUP), F32),
        in_specs=[vmem], out_specs=vmem,
        compiler_params=pltpu.CompilerParams(vmem_limit_bytes=4 * 2**20),
        name="finish",
    )(parts)


def solution(mesh):
    torus = Mesh(
        mesh.devices.reshape(4, 4, 2, mesh.shape["lat"]), ("mem_0", "mem_1", "mem_2", "lat")
    )
    in_specs = (
        P(MEM, None, "lat", None),
        P(None, "lat", MEM),
        P(None, "lat", None),
        P(None, "lat", None),
        P(None, "lat", None),
    )
    out_specs = P(None, "lat", MEM)

    return jax.shard_map(
        shards, mesh=torus, in_specs=in_specs, out_specs=out_specs, check_vma=False
    )
```

```python
import jax
import jax.numpy as jnp
from jax import lax
from jax.experimental import pallas as pl
from jax.experimental.pallas import tpu as pltpu
from jax.sharding import Mesh
from jax.sharding import PartitionSpec as P

SWEEP = 4
MEM = ("mem_0", "mem_1", "mem_2")
CHIP = ("mem_0", "mem_1")
HALO = 2 * SWEEP
GROUP = 32
LANES = 128
UNROLL = 4
CLOSED = 66_150_400
F32 = jnp.float32
BF16 = jnp.bfloat16


def splitting(length, period):
    source = lax.broadcasted_iota(jnp.int32, (length, length), 0)
    target = lax.broadcasted_iota(jnp.int32, (length, length), 1)
    return one_hot(source, target, period)


def one_hot(source, target, period):
    inner = source & (period - 1)
    moved = (source - inner) + (inner & 1) * (period // 2) + (inner >> 1)
    return (moved == target).astype(F32).astype(BF16)


def exact_dot(values, matrix):
    high = values.astype(BF16)
    rest = values - high.astype(F32)
    mid = rest.astype(BF16)
    low = (rest - mid.astype(F32)).astype(BF16)

    def dot(part):
        return jnp.dot(part, matrix, preferred_element_type=F32)

    return (dot(high) + dot(mid)) + dot(low)


def exchange(values, lane):
    values = list(values)
    width = LANES // 8
    for d in (1, 2, 4):
        is_set = (lane & (width * d)) != 0
        for i in range(8):
            if i & d:
                continue
            a, b = values[i], values[i + d]
            values[i] = jnp.where(is_set, pltpu.roll(b, width * d, 1), a)
            values[i + d] = jnp.where(is_set, b, pltpu.roll(a, LANES - width * d, 1))
    return values


def at8(j):
    return pl.ds(pl.multiple_of(j * 8, 8), 8)


def at16(j, pair):
    return pl.ds(pl.multiple_of(j * 16 + 8 * pair, 8), 8)


def neighbours(values, lane):
    even, odd = values[:4], values[4:]
    east = [pltpu.roll(v, LANES - 1, 1) for v in even]
    west = [pltpu.roll(v, 1, 1) for v in odd]
    east = [jnp.where(lane == LANES - 1, east[(t + 1) % 4], east[t]) for t in range(4)]
    west = [jnp.where(lane == 0, west[(t - 1) % 4], west[t]) for t in range(4)]
    return odd + east, west + even


def edge_kernel(gradient, perturb, k_north, k_east, scale, packed, first, last, top, bottom,
                block, narrow, wide, arrive, leave):
    rows = perturb.shape[2]
    load = pltpu.make_async_copy(gradient, block, arrive.at[2, 0])
    load.start()
    inward, outward = [], []
    for side, (out, start) in enumerate(((top, rows - HALO), (bottom, 0))):
        at = pl.ds(start, HALO)
        inward.append([
            pltpu.make_async_copy(ref.at[:, at, :], wide.at[side, pl.ds(16 + 4 * a, 4)],
                                  arrive.at[side, a])
            for a, ref in enumerate((k_north, k_east, scale))
        ] + [pltpu.make_async_copy(perturb.at[:, :, at, :], narrow.at[side], arrive.at[side, 3])])
        outward.append([
            pltpu.make_async_copy(wide.at[side, pl.ds(k, 4)], out.at[pl.ds(k, 4)],
                                  leave.at[side, k // 4])
            for k in range(0, 28, 4)
        ])
    for side in range(2):
        for copy in inward[side]:
            copy.start()
    load.wait()
    joined = jnp.concatenate([block[l] for l in range(block.shape[0])], axis=1)
    value = exact_dot(joined, splitting(LANES, GROUP))
    packed[...] = value
    first[...] = value[:HALO]
    last[...] = value[-HALO:]
    for side in range(2):
        for a in range(3):
            inward[side][a].wait()
            outward[side][4 + a].start()
    for side in range(2):
        inward[side][3].wait()
        for m in range(4):
            for l in range(4):
                wide[side, 4 * m + l] = narrow[side, m, l].astype(F32)
            outward[side][m].start()
    for side in range(2):
        for copy in outward[side]:
            copy.wait()


def finish_kernel(count, parts, out):
    total = parts[0]
    for k in range(1, parts.shape[0]):
        total = total + parts[k]
    total = total / F32(count)
    source = lax.broadcasted_iota(jnp.int32, (LANES, LANES), 1)
    target = lax.broadcasted_iota(jnp.int32, (LANES, LANES), 0)
    total = exact_dot(total, one_hot(source, target, GROUP))
    for l in range(out.shape[0]):
        out[l] = total[:, l * GROUP:(l + 1) * GROUP]


def coefficients(rows, refs, lane):
    north, east, step, to_north, to_south, to_east, to_west, centre, inverse = refs

    def one(j):
        s = [step[t, at8(j), :] for t in range(8)]
        e = [east[t, at8(j), :] for t in range(8)]
        _, w = neighbours(e, lane)
        for t in range(8):
            up = s[t] * north[t, at8(j), :]
            down = s[t] * north[t, at8(j - 1), :]
            right = s[t] * e[t]
            left = s[t] * w[t]
            to_north[t, at8(j), :] = up
            to_south[t, at8(j), :] = down
            to_east[t, at8(j), :] = right
            to_west[t, at8(j), :] = left
            centre[t, at8(j), :] = 1.0 - ((up + down) + (right + left))
            inverse[t, at8(j), :] = 1.0 / jnp.where(s[t] == 0.0, 1.0, s[t])

    def chunk(i, _):
        for k in range(UNROLL):
            one(rows[0] + i * UNROLL + k)
        return 0

    lax.fori_loop(0, (rows[1] - rows[0]) // UNROLL, chunk, 0)


def prepare_kernel(perturb_all, north_all, east_all, scale_all, member, *args):
    refs, (perturb, faces, sems) = args[:9], args[9:]
    levels, rows, width = north_all.shape
    north, east, step = refs[:3]
    halves = [
        pltpu.make_async_copy(
            perturb_all.at[:, :, :, pl.ds(k * width // 4, width // 4)],
            perturb.at[:, :, :, pl.ds(k * width // 4, width // 4)], sems.at[k],
        )
        for k in range(4)
    ]
    copies = [
        pltpu.make_async_copy(source, faces.at[a], sems.at[4 + a])
        for a, source in enumerate((north_all, east_all, scale_all))
    ]
    for copy in halves + copies:
        copy.start()
    k_north, k_east, scale = (faces.at[a] for a in range(3))
    matrix = splitting(256, 256)
    row = lax.broadcasted_iota(jnp.int32, (rows, 256), 0)
    edge = (row == rows - 1) & (lax.axis_index("lat") == lax.axis_size("lat") - 1)
    for u in range(width // 256):
        cols = slice(u * 256, (u + 1) * 256)
        halves[u].wait()
        for m in range(4):
            values = jnp.dot(
                perturb[m, :, :, cols].reshape(levels * rows, 256), matrix,
                preferred_element_type=F32,
            )
            for l in range(levels):
                at = HALO * 16 + (m // 2) * 8 + 2 * l + m % 2
                for odd in range(2):
                    member[u + 4 * odd, pl.ds(at, rows, stride=16), :] = values[
                        l * rows:(l + 1) * rows, odd * LANES:(odd + 1) * LANES
                    ]
    for copy in copies:
        copy.wait()
    for u in range(width // 256):
        cols = slice(u * 256, (u + 1) * 256)
        for ref, source in ((north, k_north), (east, k_east), (step, scale)):
            parts = [source[l, :, cols] for l in range(levels)]
            if ref is north:
                parts = [jnp.where(edge, 0.0, part) for part in parts]
            values = exact_dot(jnp.concatenate(parts, axis=0), matrix)
            for l in range(levels):
                for odd in range(2):
                    value = values[l * rows:(l + 1) * rows, odd * LANES:(odd + 1) * LANES]
                    for twin in range(2):
                        at = HALO * 8 + 2 * l + twin
                        ref[u + 4 * odd, pl.ds(at, rows, stride=8), :] = value
    lane = lax.broadcasted_iota(jnp.int32, (8, LANES), 1)
    coefficients((HALO, HALO + rows), refs, lane)


def sweep_kernel(low, high, mine, other, *args):
    keep, send = args[10:12]
    member, *refs = args[12:22]
    scratch = args[22:]
    step, (to_north, to_south, to_east, to_west, centre, inverse) = refs[2], refs[3:]
    fields, guess, total, near, sems = scratch[:2], scratch[2], scratch[3], scratch[4], scratch[5]
    rows, levels, span = keep.shape[1], 4, mine.shape[1]
    core = lax.axis_index("mem_2")
    copies = [
        pltpu.make_async_copy(source, near.at[k], sems.at[k]) for k, source in enumerate((low, high))
    ]
    for copy in copies:
        copy.start()

    for copy in copies:
        copy.wait()
    wide = lax.broadcasted_iota(jnp.int32, (span, LANES), 1)
    for u in range(4):
        blocks = []
        for k in range(8):
            chip, owner = 4 * u + k // 2, k % 2
            blocks.append(jnp.where(core == owner, mine[chip], other[chip]))
        for k, value in enumerate(exchange(blocks, wide)):
            l, odd = k // 2, k % 2
            for twin in range(2):
                guess[u + 4 * odd, pl.ds(2 * l + twin, span, stride=8), :] = value

    matrix = splitting(256, 256)
    lane = lax.broadcasted_iota(jnp.int32, (8, LANES), 1)

    for u in range(low.shape[2] // 256):
        cols = slice(u * 256, (u + 1) * 256)
        for k, first in ((0, 0), (1, HALO + rows)):
            source = near.at[k]
            values = jnp.dot(
                source[:16, :, cols].reshape(16 * HALO, 256).astype(BF16), matrix,
                preferred_element_type=F32,
            )
            for m in range(4):
                for l in range(levels):
                    at = first * 16 + (m // 2) * 8 + 2 * l + m % 2
                    at_row = (m * levels + l) * HALO
                    for odd in range(2):
                        member[u + 4 * odd, pl.ds(at, HALO, stride=16), :] = values[
                            at_row:at_row + HALO, odd * LANES:(odd + 1) * LANES
                        ]
            values = exact_dot(source[16:, :, cols].reshape(12 * HALO, 256), matrix)
            for a in range(3):
                for l in range(levels):
                    at_row = (a * levels + l) * HALO
                    for odd in range(2):
                        for twin in range(2):
                            at = first * 8 + 2 * l + twin
                            refs[a][u + 4 * odd, pl.ds(at, HALO, stride=8), :] = values[
                                at_row:at_row + HALO, odd * LANES:(odd + 1) * LANES
                            ]
    for t in range(8):
        last = (t, at8(HALO - 1), slice(None))
        refs[0][last] = jnp.where(lax.axis_index("lat") == 0, 0.0, refs[0][last])
    coefficients((1, HALO + 1), refs, lane)
    coefficients((HALO + rows, span), refs, lane)

    def start(i, _):
        for k in range(UNROLL):
            j = i * UNROLL + k
            for t in range(8):
                scaled = step[t, at8(j), :] * guess[t, at8(j), :]
                for pair in range(2):
                    fields[0][t, at16(j, pair), :] = member[t, at16(j, pair), :] * scaled
        return 0

    lax.fori_loop(0, span // UNROLL, start, 0)

    def advance(source, target, first, count, finish, last):
        def chunk(begin, length):
            for k in range(length):
                j = begin + k
                terms = [None] * 8
                for pair in range(2):
                    here = [source[t, at16(j, pair), :] for t in range(8)]
                    right, left = neighbours(here, lane)
                    for t in range(8):
                        value = centre[t, at8(j), :] * here[t]
                        value += to_north[t, at8(j), :] * source[t, at16(j + 1, pair), :]
                        value += to_south[t, at8(j), :] * source[t, at16(j - 1, pair), :]
                        side = to_east[t, at8(j), :] * right[t] + to_west[t, at8(j), :] * left[t]
                        value += side
                        if finish:
                            value = value * inverse[t, at8(j), :]
                        if not last:
                            target[t, at16(j, pair), :] = value
                        else:
                            term = member[t, at16(j, pair), :] * value
                            terms[t] = term if pair == 0 else terms[t] + term
                if last:
                    for t in range(8):
                        total[t, at8(j - HALO), :] = terms[t]
            return 0

        whole = count // (2 * UNROLL)
        lax.fori_loop(0, whole, lambda i, _: chunk(first + i * 2 * UNROLL, 2 * UNROLL), 0)
        if count % (2 * UNROLL):
            chunk(first + whole * 2 * UNROLL, count % (2 * UNROLL))

    for n in range(2 * SWEEP):
        advance(fields[n % 2], fields[1 - n % 2], n + 1, span - 2 * n - 2,
                n == SWEEP - 1, n == 2 * SWEEP - 1)
    wide = lax.broadcasted_iota(jnp.int32, (rows, LANES), 1)
    for u in range(4):
        sums = []
        for k in range(8):
            l, t = k // 2, u + 4 * (k % 2)
            sums.append(
                total[t, pl.ds(2 * l, rows, stride=8), :]
                + total[t, pl.ds(2 * l + 1, rows, stride=8), :]
            )
        blocks = exchange(sums, wide)
        for k in range(4):
            a, b = blocks[2 * k], blocks[2 * k + 1]
            keep[4 * u + k] = jnp.where(core == 0, a, b)
            send[4 * u + k] = jnp.where(core == 0, b, a)


def shards(perturb, gradient, k_north, k_east, scale):
    members, levels, rows, width = perturb.shape
    span = rows + 2 * HALO
    size = lax.axis_size("lat")
    up = [(i, (i + 1) % size) for i in range(size)]
    down = [(j, i) for i, j in up]
    swap = [(0, 1), (1, 0)]
    vmem = pl.BlockSpec(memory_space=pltpu.VMEM)
    hbm = pl.BlockSpec(memory_space=pltpu.HBM)

    rim = jax.ShapeDtypeStruct((HALO, LANES), F32)
    edges = jax.ShapeDtypeStruct((7 * levels, HALO, width), F32)
    packed, first, last, top, bottom = pl.pallas_call(
        edge_kernel,
        out_shape=[jax.ShapeDtypeStruct((rows, LANES), F32), rim, rim, edges, edges],
        in_specs=[hbm] * 5, out_specs=[vmem] * 3 + [hbm] * 2,
        scratch_shapes=[
            pltpu.VMEM(gradient.shape, F32),
            pltpu.VMEM((2, 4, levels, HALO, width), BF16),
            pltpu.VMEM((2, 7 * levels, HALO, width), F32),
            pltpu.SemaphoreType.DMA((3, 4)),
            pltpu.SemaphoreType.DMA((2, 7)),
        ],
        compiler_params=pltpu.CompilerParams(vmem_limit_bytes=CLOSED),
        name="edges",
    )(gradient, perturb, k_north, k_east, scale)
    below = lax.ppermute(last, "lat", up)
    above = lax.ppermute(first, "lat", down)
    low = lax.ppermute(top, "lat", up)
    high = lax.ppermute(bottom, "lat", down)

    chips = lax.axis_size(CHIP)
    block = jnp.concatenate([below, packed, above], axis=0)
    spread = jnp.broadcast_to(block[None], (chips, span, LANES))
    mine = lax.all_to_all(spread, CHIP, 0, 0, tiled=True)
    other = lax.ppermute(mine, "mem_2", swap)

    padded = span + UNROLL
    tall = pltpu.VMEM((8, padded * 16, LANES), F32)
    short = pltpu.VMEM((8, padded * 8, LANES), F32)
    prepare = pl.pallas_call(
        prepare_kernel,
        out_shape=[tall] + [short] * 9,
        in_specs=[hbm] * 4,
        out_specs=[vmem] * 10,
        scratch_shapes=[
            pltpu.VMEM(perturb.shape, BF16),
            pltpu.VMEM((3,) + k_north.shape, F32),
            pltpu.SemaphoreType.DMA((7,)),
        ],
        compiler_params=pltpu.CompilerParams(vmem_limit_bytes=44 * 2**20),
        cost_estimate=pl.CostEstimate(flops=0, bytes_accessed=24 * 2**20, transcendentals=0),
        name="prepare",
    )
    prepared = prepare(perturb, k_north, k_east, scale)

    part = jax.ShapeDtypeStruct((chips, rows, LANES), F32)
    keep, send = pl.pallas_call(
        sweep_kernel,
        out_shape=[part, part] + [tall] + [short] * 9,
        in_specs=[hbm] * 2 + [vmem] * 12,
        out_specs=[vmem] * 12,
        input_output_aliases={4 + k: 2 + k for k in range(10)},
        scratch_shapes=[
            tall,
            tall,
            pltpu.VMEM((8, span * 8, LANES), F32),
            pltpu.VMEM((8, rows * 8, LANES), F32),
            pltpu.VMEM((2, 7 * levels, HALO, width), F32),
            pltpu.SemaphoreType.DMA((2,)),
        ],
        compiler_params=pltpu.CompilerParams(vmem_limit_bytes=18 * 2**20),
        name="sweeps",
    )(low, high, mine, other, *prepared)[:2]

    merged = keep + lax.ppermute(send, "mem_2", swap)
    parts = lax.all_to_all(merged, CHIP, 0, 0, tiled=True)
    count = members * lax.axis_size(MEM) - 1
    return pl.pallas_call(
        lambda p, o: finish_kernel(count, p, o),
        out_shape=jax.ShapeDtypeStruct((levels, rows, GROUP), F32),
        in_specs=[vmem], out_specs=vmem,
        compiler_params=pltpu.CompilerParams(vmem_limit_bytes=4 * 2**20),
        name="finish",
    )(parts)


def solution(mesh):
    torus = Mesh(
        mesh.devices.reshape(4, 4, 2, mesh.shape["lat"]), ("mem_0", "mem_1", "mem_2", "lat")
    )
    in_specs = (
        P(MEM, None, "lat", None),
        P(None, "lat", MEM),
        P(None, "lat", None),
        P(None, "lat", None),
        P(None, "lat", None),
    )
    out_specs = P(None, "lat", MEM)

    return jax.shard_map(
        shards, mesh=torus, in_specs=in_specs, out_specs=out_specs, check_vma=False
    )
```
